32 devices in a mesh: clus: 8 (over y, x, core), head: 4 (over z).
Axes of the slice: x: 2, y: 2, z: 4, core: 2. Of those that a mesh axis runs over, the one named last changes fastest.
Arguments:
- node_queries: bfloat16 [32768, 1024], P(('clus', 'head')), may hold values from -8 to 8
- node_keys: bfloat16 [32768, 1024], P(('clus', 'head')), may hold values from -8 to 8
- node_values: bfloat16 [32768, 1024], P(('clus', 'head')), may hold values from -6 to 6
- matchings: int32 [3, 8], replicated, may hold values from 0 to 7, as said below
- patterns: int32 [8, 32, 12], P('clus'), may hold values from 0 to 127, as said below
- out_gain: float32 [1024], replicated, may hold values from 0.5 to 1.5
Outputs:
- attended: bfloat16 [32768, 1024], P(('clus', 'head'))
The draws below stay inside these ranges and needn't reach their ends.
Inputs may be any that keep to these rules, and one draw needn't show every extreme that they name: Each row is a perfect matching: matchings[j, c] != c and matchings[j, matchings[j, c]] == c. `patterns`: for every cluster and query block, entries s * 3 to (s + 1) * 3 - 1 are 3 different blocks of source s, that is numbers from s * 32 to (s + 1) * 32 - 1.
All inputs are finite; a program needn't handle non-finite values.
Results may differ from the reference program's by a relative error of at most 0.0057.
Values may be sent and summed in bfloat16 or wider, within the bound.
No kernel may reach another device: no remote copies, remote signals or barrier semaphores. Data moves between devices by JAX's collectives and lax.ppermute only.
A program may use at most 128 MiB of HBM per device.

```python
import math
import jax
import jax.numpy as jnp
from jax import lax

D = 1024
HEAD_DIM = 64
CN = 4096
BLOCK = 128
PER_SRC = 3
MATCHINGS = 3
CLUSTERS = 8
NODES = 32768
BLOCKS = 32
NB = 12


def draw_node_queries(key, part):
    normal_draw = jax.random.normal(jax.random.fold_in(key, 21), (NODES, D), jnp.float32)
    return jnp.clip(normal_draw, -6.0, 6.0).astype(jnp.bfloat16)


def draw_node_keys(key, part):
    normal_draw = jax.random.normal(jax.random.fold_in(key, 31), (NODES, D), jnp.float32)
    return jnp.clip(normal_draw, -6.0, 6.0).astype(jnp.bfloat16)


def draw_matchings(key, part):
    rows_out = []
    for which in range(MATCHINGS):
        shuffled = jax.random.permutation(jax.random.fold_in(key, 41 + which), CLUSTERS).astype(jnp.int32)
        first_half = shuffled[0::2]
        second_half = shuffled[1::2]
        partner = jnp.zeros((CLUSTERS,), jnp.int32).at[first_half].set(second_half).at[second_half].set(first_half)
        rows_out.append(partner)
    return jnp.stack(rows_out)


def draw_patterns(key, part):
    total = CLUSTERS * BLOCKS * (MATCHINGS + 1)
    subkeys = jax.random.split(jax.random.fold_in(key, 51), total)
    picks = jax.vmap(lambda subkey: jax.random.permutation(subkey, BLOCKS)[:PER_SRC])(subkeys)
    picks = picks.reshape(CLUSTERS, BLOCKS, MATCHINGS + 1, PER_SRC).astype(jnp.int32)
    offsets = (jnp.arange(MATCHINGS + 1, dtype=jnp.int32) * BLOCKS)[None, None, :, None]
    return (picks + offsets).reshape(CLUSTERS, BLOCKS, NB)


def steps_of(key, extent, cuts, least, largest):
    factor_of = 1.0
    for axis_at, shards_of in cuts:
        steps = jax.random.uniform(jax.random.fold_in(jax.random.fold_in(key, 6), axis_at), (shards_of,), jnp.float32, least / len(cuts), largest / len(cuts))
        factor_of = factor_of * jnp.repeat(jnp.exp(steps), extent[axis_at] // shards_of).reshape((-1,) + (1,) * (len(extent) - 1 - axis_at))
    return factor_of


def noise(rng, shape, width, bound, pieces=(), held_as=jnp.bfloat16):
    values = width * jax.random.normal(rng, shape, jnp.float32)
    if pieces:
        values = values * steps_of(rng, shape, pieces, -0.22, 0.18)
    return jnp.clip(values, -bound, bound).astype(held_as)


def setup_inputs(seed: int = 0) -> dict:
    arg_keys = jax.random.split(jax.random.key(seed), 7)
    node_queries = draw_node_queries(jax.random.fold_in(arg_keys[6], 71), 0)
    node_keys = draw_node_keys(jax.random.fold_in(arg_keys[6], 71), 0)
    node_values = noise(arg_keys[2], (NODES, D), 1.0, 6.0, ((0, 32),))
    matchings = draw_matchings(jax.random.fold_in(arg_keys[6], 71), 0)
    patterns = draw_patterns(jax.random.fold_in(arg_keys[6], 71), 0)
    out_gain = jnp.clip(1.0 + 0.1 * jax.random.normal(arg_keys[5], (D,), jnp.float32), 0.5, 1.5)
    return dict(node_queries=node_queries, node_keys=node_keys, node_values=node_values, matchings=matchings, patterns=patterns, out_gain=out_gain)


group_blocks = 4

def attend_group(query_group, key_group, value_group):
    score_scale = 1.0 / math.sqrt(HEAD_DIM)
    scores = jnp.einsum('bqhd,bkhd->bhqk', query_group.astype(jnp.float32), key_group.astype(jnp.float32)) * score_scale
    maximum = lax.optimization_barrier(jnp.max(scores, axis=-1, keepdims=True))
    powers = jnp.exp(scores - maximum)
    weights = (powers / lax.optimization_barrier(jnp.sum(powers, axis=-1, keepdims=True))).astype(jnp.bfloat16)
    mixed_rows = jnp.einsum('bhqk,bkhd->bqhd', weights.astype(jnp.float32), value_group.astype(jnp.float32))
    return mixed_rows.astype(jnp.bfloat16)

def attend_cluster(query_rows, key_rows, value_rows, pattern):
    row_count = query_rows.shape[0]
    feature_width = query_rows.shape[1]
    head_count = feature_width // HEAD_DIM
    groups = pattern.shape[0] // group_blocks
    query_groups = query_rows.reshape(groups, group_blocks, BLOCK, head_count, HEAD_DIM)
    key_blocks = key_rows.reshape(-1, BLOCK, head_count, HEAD_DIM)
    value_blocks = value_rows.reshape(-1, BLOCK, head_count, HEAD_DIM)
    pattern_groups = pattern.reshape(groups, group_blocks, -1)

    def one_group(inputs):
        query_group, chosen = inputs
        key_group = jnp.take(key_blocks, chosen, axis=0).reshape(group_blocks, -1, head_count, HEAD_DIM)
        value_group = jnp.take(value_blocks, chosen, axis=0).reshape(group_blocks, -1, head_count, HEAD_DIM)
        return attend_group(query_group, key_group, value_group)
    mixed_rows = lax.map(one_group, (query_groups, pattern_groups))
    return mixed_rows.reshape(row_count, feature_width)

def reference(node_queries, node_keys, node_values, matchings, patterns, out_gain):
    cluster_queries = node_queries.reshape(CLUSTERS, CN, D)
    cluster_keys = node_keys.reshape(CLUSTERS, CN, D)
    cluster_values = node_values.reshape(CLUSTERS, CN, D)

    def one_cluster(cluster):
        partners = matchings[:, cluster]
        key_rows = jnp.concatenate([cluster_keys[cluster][None], jnp.take(cluster_keys, partners, axis=0)], axis=0).reshape(-1, D)
        value_rows = jnp.concatenate([cluster_values[cluster][None], jnp.take(cluster_values, partners, axis=0)], axis=0).reshape(-1, D)
        return attend_cluster(cluster_queries[cluster], key_rows, value_rows, patterns[cluster])
    mixed_rows = lax.map(one_cluster, jnp.arange(CLUSTERS, dtype=jnp.int32))
    mixed_rows = mixed_rows.reshape(-1, D).astype(jnp.float32)
    mean_square = lax.optimization_barrier(jnp.mean(mixed_rows * mixed_rows, axis=-1, keepdims=True))
    return (mixed_rows * lax.rsqrt(mean_square + 1e-06) * out_gain.astype(jnp.float32)).astype(jnp.bfloat16)
```

```python
import functools
import math

import jax
import jax.numpy as jnp
from jax import lax
from jax.experimental import pallas as pl
from jax.experimental.pallas import tpu as pltpu
from jax.sharding import PartitionSpec as P

HEAD_DIM = 64
LANES = 128


def swap(array, axis, size, flip):
    return lax.ppermute(array, axis, [(i, i ^ flip) for i in range(size)])


def split_kernel(ranks, cores, width, at, keys, values, queries, *rest):
    outs, sem = rest[:-1], rest[-1]
    pairs, heads = outs[:cores], outs[cores:]
    core, rank = at[0], at[1]
    copies = []
    for which in range(cores):
        for flip in range(ranks):
            column = ((rank ^ flip) * cores + (core ^ which)) * width
            columns = pl.ds(pl.multiple_of(column, width), width)
            copies += [
                pltpu.make_async_copy(
                    keys.at[:, columns], pairs[which].at[flip, :, pl.ds(0, width)], sem
                ),
                pltpu.make_async_copy(
                    values.at[:, columns], pairs[which].at[flip, :, pl.ds(width, width)], sem
                ),
                pltpu.make_async_copy(queries.at[:, columns], heads[which].at[flip], sem),
            ]
    for copy in copies:
        copy.start()
    for copy in copies:
        copy.wait()


def split_heads(queries, keys, values, core, rank, ranks, cores, width):
    rows = queries.shape[0]
    if width % LANES == 0:
        hbm = pl.BlockSpec(memory_space=pl.ANY)
        outs = pl.pallas_call(
            functools.partial(split_kernel, ranks, cores, width),
            grid_spec=pltpu.PrefetchScalarGridSpec(
                num_scalar_prefetch=1,
                grid=(1,),
                in_specs=[hbm] * 3,
                out_specs=[hbm] * (2 * cores),
                scratch_shapes=[pltpu.SemaphoreType.DMA],
            ),
            out_shape=[jax.ShapeDtypeStruct((ranks, rows, 2 * width), keys.dtype)] * cores
            + [jax.ShapeDtypeStruct((ranks, rows, width), keys.dtype)] * cores,
            name="split_heads",
        )(jnp.stack([core, rank]), keys, values, queries)
        return outs[:cores], outs[cores:]
    order = rank ^ jnp.arange(ranks)

    def pieces(array):
        return jnp.moveaxis(array.reshape(rows, ranks, cores, width), 0, 2)[order]

    cut_keys, cut_values, cut_queries = pieces(keys), pieces(values), pieces(queries)
    pair = jnp.concatenate([cut_keys, cut_values], axis=-1)
    which = [core ^ i for i in range(cores)]
    return [jnp.take(pair, i, axis=1) for i in which], [
        jnp.take(cut_queries, i, axis=1) for i in which
    ]


def attend_kernel(counts, width, table, queries, *rest):
    pieces = rest[: len(counts)]
    mixed, held, sem = rest[len(counts) :]
    step = pl.program_id(0)
    block = queries.shape[0]
    heads = width // HEAD_DIM
    picks = table.shape[1]

    @pl.when(step == 0)
    def _():
        copies = []
        start = 0
        for piece, count in zip(pieces, counts):
            copies.append(pltpu.make_async_copy(piece, held.at[pl.ds(start, count)], sem))
            start += count
        for copy in copies:
            copy.start()
        for copy in copies:
            copy.wait()

    pair = jnp.concatenate([held[table[step, i]] for i in range(picks)], axis=0)
    query = queries[...]
    zero = jnp.zeros((), query.dtype)
    if width % LANES == 0:
        key, value = pair[:, :width], pair[:, width:]
        lane = lax.broadcasted_iota(jnp.int32, (block, width), 1) // HEAD_DIM
        stacked = jnp.concatenate(
            [jnp.where(lane == head, query, zero) for head in range(heads)], axis=0
        )
    else:
        key = value = pair
        stacked = jnp.concatenate([query, jnp.zeros_like(query)], axis=1)
    scores = lax.dot_general(
        stacked, key, (((1,), (1,)), ((), ())), preferred_element_type=jnp.float32
    )
    maximum = jnp.max(scores, axis=1, keepdims=True)
    powers = jnp.exp2((scores - maximum) * (math.log2(math.e) / math.sqrt(HEAD_DIM)))
    total = jnp.sum(powers, axis=1, keepdims=True)
    summed = jnp.dot(powers.astype(value.dtype), value, preferred_element_type=jnp.float32)
    summed = summed / total
    if width % LANES == 0:
        result = summed[:block]
        for head in range(1, heads):
            result = jnp.where(lane == head, summed[head * block : (head + 1) * block], result)
    else:
        result = summed[:, width:]
    mixed[...] = result.astype(mixed.dtype)


def attend(table, queries, pieces, block, width):
    steps = table.shape[0]
    blocks = [piece.reshape(-1, block, piece.shape[-1]) for piece in pieces]
    counts = tuple(piece.shape[0] for piece in blocks)
    return pl.pallas_call(
        functools.partial(attend_kernel, counts, width),
        grid_spec=pltpu.PrefetchScalarGridSpec(
            num_scalar_prefetch=1,
            grid=(steps,),
            in_specs=[pl.BlockSpec((block, width), lambda i, t: (i, 0))]
            + [pl.BlockSpec(memory_space=pl.ANY)] * len(blocks),
            out_specs=pl.BlockSpec((block, width), lambda i, t: (i, 0)),
            scratch_shapes=[
                pltpu.VMEM((sum(counts), block, blocks[0].shape[-1]), queries.dtype),
                pltpu.SemaphoreType.DMA,
            ],
        ),
        out_shape=jax.ShapeDtypeStruct(queries.shape, queries.dtype),
        name="attend",
    )(table, queries, *blocks)


def norm_kernel(cores, width, at, *rest):
    pieces, gain, out = rest[:-2], rest[-2], rest[-1]
    core, rank = at[0], at[1]
    parts = []
    square = 0.0
    for flip in range(len(pieces) // cores):
        for which in range(cores):
            part = pieces[flip * cores + which][0].astype(jnp.float32)
            square = square + part * part
            parts.append((((rank ^ flip) * cores + (core ^ which)) * width, part))
    features = len(parts) * width
    mean_square = jnp.sum(square, axis=-1, keepdims=True) * (1.0 / features)
    factor = lax.rsqrt(mean_square + 1e-06)
    for column, part in parts:
        columns = pl.ds(pl.multiple_of(column, width), width)
        out[:, columns] = (part * factor * gain[:, columns]).astype(out.dtype)


def normalize(own, other, gain, core, rank, cores, width):
    ranks = len(own)
    rows = own[0].shape[1]
    if width % LANES == 0:
        step = min(rows, 256)
        specs, operands = [], []
        for flip in range(ranks):
            specs.append(pl.BlockSpec((1, step, width), lambda i, t: (0, i, 0)))
            operands.append(own[flip])
            if cores > 1:
                specs.append(
                    pl.BlockSpec((1, step, width), functools.partial(lambda f, i, t: (f, i, 0), flip))
                )
                operands.append(other)
        features = ranks * cores * width
        return pl.pallas_call(
            functools.partial(norm_kernel, cores, width),
            grid_spec=pltpu.PrefetchScalarGridSpec(
                num_scalar_prefetch=1,
                grid=(rows // step,),
                in_specs=specs + [pl.BlockSpec((1, features), lambda i, t: (0, 0))],
                out_specs=pl.BlockSpec((step, features), lambda i, t: (i, 0)),
            ),
            out_shape=jax.ShapeDtypeStruct((rows, features), own[0].dtype),
            name="normalize",
        )(jnp.stack([core, rank]), *operands, gain[None])
    order = rank ^ jnp.arange(ranks)
    stacked = jnp.stack([piece[0] for piece in own])[None]
    if cores > 1:
        stacked = jnp.concatenate([stacked, other[None]], axis=0)[core ^ jnp.arange(cores)]
    restored = jnp.transpose(stacked[:, order], (2, 1, 0, 3)).reshape(rows, -1)
    restored = restored.astype(jnp.float32)
    mean_square = jnp.mean(restored * restored, axis=-1, keepdims=True)
    return (restored * lax.rsqrt(mean_square + 1e-06) * gain).astype(own[0].dtype)


def local(clusters, ranks, queries, keys, values, matchings, patterns, gain):
    rows, features = queries.shape
    heads = features // HEAD_DIM // ranks
    cores = 2 if heads % 2 == 0 and clusters % 2 == 0 else 1
    width = heads // cores * HEAD_DIM
    at = lax.axis_index("clus")
    core, rank = at % cores, lax.axis_index("head")
    blocks = patterns.shape[1]
    block = rows * ranks // blocks
    rank_blocks = rows // block

    pairs, heads_of = split_heads(queries, keys, values, core, rank, ranks, cores, width)
    if cores > 1:
        pair_other = swap(pairs[1], "clus", clusters, 1)
        query_other = swap(heads_of[1], "clus", clusters, 1)
        pattern_other = swap(patterns, "clus", clusters, 1)
        pair_own = [jnp.stack([pairs[0][i], pair_other[i]]) for i in range(ranks)]
        query_own = [jnp.stack([heads_of[0][i], query_other[i]]) for i in range(ranks)]
        chosen = jnp.concatenate([patterns, pattern_other], axis=0)
    else:
        pair_own = [pairs[0][i][None] for i in range(ranks)]
        query_own = [heads_of[0][i][None] for i in range(ranks)]
        chosen = patterns

    pair_own = [
        piece if flip == 0 else swap(piece, "head", ranks, flip)
        for flip, piece in enumerate(pair_own)
    ]
    query_own = [
        piece if flip == 0 else swap(piece, "head", ranks, flip)
        for flip, piece in enumerate(query_own)
    ]

    bits = [cores << i for i in range((clusters // cores).bit_length() - 1)]
    span = max(1, ranks // 4)
    streams = []
    for number, start in enumerate(range(0, ranks, span)):
        group = pair_own[start : start + span]
        stream = jnp.stack(group) if span > 1 else group[0][None]
        gathered = {0: stream}
        for bit in bits if number % 2 == 0 else bits[::-1]:
            gathered |= {
                there | bit: swap(piece, "clus", clusters, bit)
                for there, piece in gathered.items()
            }
        streams.append([gathered[there] for there in sorted(gathered)])
    pieces = [piece for stream in streams for piece in stream]

    source, number = chosen // blocks, chosen % blocks
    clusters_of = at ^ jnp.arange(cores)
    sources = jnp.concatenate([clusters_of[None], matchings[:, clusters_of]], axis=0)
    partner = jnp.take_along_axis(
        sources.T[:, None, :], source, axis=2
    )
    there = partner ^ at
    flip = (number // rank_blocks) ^ rank
    place = (flip // span) * (clusters // cores) + there // cores
    place = ((place * span + flip % span) * cores + there % cores) * rank_blocks
    place = place + number % rank_blocks
    table = place.reshape(cores, ranks, rank_blocks, -1)[:, rank ^ jnp.arange(ranks)]
    table = jnp.swapaxes(table, 0, 1).reshape(ranks * cores * rank_blocks, -1)

    stacked = jnp.concatenate([piece.reshape(-1, width) for piece in query_own], axis=0)
    mixed = attend(table.astype(jnp.int32), stacked, pieces, block, width)
    mixed = mixed.reshape(ranks, cores, rows, width)
    own = [
        mixed[flip] if flip == 0 else swap(mixed[flip], "head", ranks, flip)
        for flip in range(ranks)
    ]
    other = None
    if cores > 1:
        other = swap(jnp.stack([piece[1] for piece in own]), "clus", clusters, 1)
    return normalize(own, other, gain, core, rank, cores, width)


def solution(mesh):
    in_specs = (
        P(("clus", "head"), None),
        P(("clus", "head"), None),
        P(("clus", "head"), None),
        P(),
        P("clus", None, None),
        P(),
    )
    out_specs = P(("clus", "head"), None)
    return jax.shard_map(
        functools.partial(local, mesh.shape["clus"], mesh.shape["head"]),
        mesh=mesh,
        in_specs=in_specs,
        out_specs=out_specs,
        check_vma=False,
    )
```

```python
import functools
import math

import jax
import jax.numpy as jnp
from jax import lax
from jax.experimental import pallas as pl
from jax.experimental.pallas import tpu as pltpu
from jax.sharding import PartitionSpec as P


HEAD_DIM = 64
LANES = 128
SCALE = math.log2(math.e) / math.sqrt(HEAD_DIM)


def swap(array, shape, cluster_flip, rank_flip):
    clusters, ranks = shape
    flip = cluster_flip * ranks + rank_flip
    return lax.ppermute(array, ("clus", "head"), [(i, i ^ flip) for i in range(clusters * ranks)])


def split_kernel(ranks, cores, width, fast, at, queries, keys, values, *outs):
    count = ranks * cores
    pairs, heads = outs[:count], outs[count:]
    core, rank = at[0], at[1]
    rows = queries.shape[0]
    for which in range(cores):
        for flip in range(ranks):
            column = ((rank ^ flip) * cores + (core ^ which)) * width
            columns = pl.ds(pl.multiple_of(column, width), width)
            pair = pairs[which * ranks + flip]
            pair[:, :width] = keys[:, columns]
            if fast:
                for start in range(0, rows, LANES):
                    pair[start : start + LANES, width:] = values[start : start + LANES, columns].T
            else:
                pair[:, width:] = values[:, columns]
            heads[which * ranks + flip][...] = queries[:, columns]


def split_heads(queries, keys, values, core, rank, ranks, cores, width, fast):
    rows, features = queries.shape
    count = ranks * cores
    if width % LANES == 0:
        step = min(rows, 256)
        outs = pl.pallas_call(
            functools.partial(split_kernel, ranks, cores, width, fast),
            grid_spec=pltpu.PrefetchScalarGridSpec(
                num_scalar_prefetch=1,
                grid=(rows // step,),
                in_specs=[pl.BlockSpec((step, features), lambda i, t: (i, 0))] * 3,
                out_specs=[pl.BlockSpec((step, 2 * width), lambda i, t: (i, 0))] * count
                + [pl.BlockSpec((step, width), lambda i, t: (i, 0))] * count,
            ),
            out_shape=[jax.ShapeDtypeStruct((rows, 2 * width), keys.dtype)] * count
            + [jax.ShapeDtypeStruct((rows, width), keys.dtype)] * count,
            name="split_heads",
        )(jnp.stack([core, rank]), queries, keys, values)
        rows_of = [outs[i * ranks : (i + 1) * ranks] for i in range(2 * cores)]
        return rows_of[:cores], rows_of[cores:]

    def pieces(array):
        return jnp.moveaxis(array.reshape(rows, ranks, cores, width), 0, 2)[
            rank ^ jnp.arange(ranks)
        ]

    cut_keys, cut_values, cut_queries = pieces(keys), pieces(values), pieces(queries)
    pair = jnp.concatenate([cut_keys, cut_values], axis=-1)
    which = [core ^ i for i in range(cores)]
    return [list(jnp.take(pair, i, axis=1)) for i in which], [
        list(jnp.take(cut_queries, i, axis=1)) for i in which
    ]


def hold_kernel(places, *refs):
    pieces, held, sem = refs[: len(places)], refs[-2], refs[-1]
    copies = [
        pltpu.make_async_copy(piece, held.at[pl.ds(place, piece.shape[0])], sem)
        for piece, place in zip(pieces, places)
    ]
    for copy in copies:
        copy.start()
    for copy in copies:
        copy.wait()


def hold(pieces, places, held, blocks):
    shape = (blocks,) + pieces[0].shape[1:]
    hbm = pl.BlockSpec(memory_space=pl.ANY)
    vmem = pl.BlockSpec(memory_space=pltpu.VMEM)
    fresh = held is None
    operands = list(pieces)
    if not fresh:
        operands.append(pltpu.with_memory_space_constraint(held, pltpu.VMEM))
    return pl.pallas_call(
        functools.partial(hold_kernel, places),
        in_specs=[hbm] * len(pieces) + ([] if fresh else [vmem]),
        out_specs=vmem,
        out_shape=pltpu.VMEM(shape, pieces[0].dtype),
        scratch_shapes=[pltpu.SemaphoreType.DMA],
        input_output_aliases={} if fresh else {len(pieces): 0},
        compiler_params=pltpu.CompilerParams(vmem_limit_bytes=20 << 20),
        name="hold",
    )(*operands)


def score_queries(query):
    block, width = query.shape
    lane = lax.broadcasted_iota(jnp.int32, (block, width), 1) // HEAD_DIM
    zero = jnp.zeros((), query.dtype)
    return jnp.concatenate(
        [jnp.where(lane == head, query, zero) for head in range(width // HEAD_DIM)], axis=0
    )


def attend_kernel(flip, blocks, at, table, query0, query1, held, out0, out1, *scratch):
    scores, peaks, weights = scratch[:2], scratch[2:4], scratch[4]
    step, steps = pl.program_id(0), pl.num_programs(0)
    block, width = out0.shape
    heads = width // HEAD_DIM
    picks = table.shape[1]
    chunk = 2 * block
    first = (at[1] ^ flip) * steps
    queries, outs = (query0, query1), (out0, out1)

    def query_of(which, number):
        return score_queries(
            queries[which][pl.ds(pl.multiple_of(number * block, block), block), :]
        )

    def score(which, number, query, part):
        row = which * blocks + first + number
        keys = jnp.concatenate(
            [held[table[row, 2 * part + i], :, :width] for i in range(2)], axis=0
        )
        made = lax.dot_general(
            keys, query, (((1,), (1,)), ((), ())), preferred_element_type=jnp.float32
        )
        scores[which][part * chunk : (part + 1) * chunk] = made
        return made.reshape(chunk // 8, 8, -1).max(0)

    @pl.when(step == 0)
    def _():
        query = query_of(0, 0)
        peak = score(0, 0, query, 0)
        for part in range(1, picks // 2):
            peak = jnp.maximum(peak, score(0, 0, query, part))
        peaks[0][...] = peak

    for which in range(2):
        other = 1 - which
        number = step if which == 0 else jnp.minimum(step + 1, steps - 1)
        query = query_of(other, number)
        maximum = jnp.max(peaks[which][...], axis=0, keepdims=True)
        peak = total = None
        for part in range(picks // 2):
            made = score(other, number, query, part)
            peak = made if peak is None else jnp.maximum(peak, made)
            span = slice(part * chunk, (part + 1) * chunk)
            powers = jnp.exp2((scores[which][span] - maximum) * SCALE)
            sums = powers.reshape(chunk // 8, 8, -1).sum(0)
            total = sums if total is None else total + sums
            weights[span] = powers.astype(weights.dtype)
        peaks[other][...] = peak
        row = which * blocks + first + step
        values = jnp.concatenate([held[table[row, i], :, width:] for i in range(picks)], axis=1)
        summed = jnp.dot(values, weights[...], preferred_element_type=jnp.float32)
        summed = summed * (1.0 / jnp.sum(total, axis=0, keepdims=True))
        own = [
            summed[head * HEAD_DIM : (head + 1) * HEAD_DIM, head * block : (head + 1) * block]
            for head in range(heads)
        ]
        outs[which][...] = jnp.concatenate(own, axis=0).T.astype(out0.dtype)


def attend(at, table, queries, held, flip, blocks):
    rows, width = queries[0].shape
    block = held.shape[1]
    picks = table.shape[1]
    whole = pl.BlockSpec(memory_space=pltpu.VMEM)
    own = pl.BlockSpec((block, width), lambda i, a, t: (i, 0))
    tall = (picks * block, width // HEAD_DIM * block)
    return pl.pallas_call(
        functools.partial(attend_kernel, flip, blocks),
        grid_spec=pltpu.PrefetchScalarGridSpec(
            num_scalar_prefetch=2,
            grid=(rows // block,),
            in_specs=[whole] * 3,
            out_specs=[own] * 2,
            scratch_shapes=[pltpu.VMEM(tall, jnp.float32)] * 2
            + [pltpu.VMEM((8, tall[1]), jnp.float32)] * 2
            + [pltpu.VMEM(tall, queries[0].dtype)],
        ),
        out_shape=[jax.ShapeDtypeStruct((rows, width), queries[0].dtype)] * 2,
        compiler_params=pltpu.CompilerParams(vmem_limit_bytes=28 << 20),
        name="attend",
    )(at, table, *queries, pltpu.with_memory_space_constraint(held, pltpu.VMEM))


def gather_attend_kernel(counts, width, table, queries, *rest):
    pieces = rest[: len(counts)]
    mixed, held, sem = rest[len(counts) :]
    step = pl.program_id(0)
    block = queries.shape[0]
    heads = width // HEAD_DIM
    picks = table.shape[1]

    @pl.when(step == 0)
    def _():
        copies = []
        start = 0
        for piece, count in zip(pieces, counts):
            copies.append(pltpu.make_async_copy(piece, held.at[pl.ds(start, count)], sem))
            start += count
        for copy in copies:
            copy.start()
        for copy in copies:
            copy.wait()

    pair = jnp.concatenate([held[table[step, i]] for i in range(picks)], axis=0)
    query = queries[...]
    zero = jnp.zeros((), query.dtype)
    if width % LANES == 0:
        key, value = pair[:, :width], pair[:, width:]
        lane = lax.broadcasted_iota(jnp.int32, (block, width), 1) // HEAD_DIM
        stacked = jnp.concatenate(
            [jnp.where(lane == head, query, zero) for head in range(heads)], axis=0
        )
    else:
        key = value = pair
        stacked = jnp.concatenate([query, jnp.zeros_like(query)], axis=1)
    scores = lax.dot_general(
        stacked, key, (((1,), (1,)), ((), ())), preferred_element_type=jnp.float32
    )
    maximum = jnp.max(scores, axis=1, keepdims=True)
    powers = jnp.exp2((scores - maximum) * (math.log2(math.e) / math.sqrt(HEAD_DIM)))
    total = jnp.sum(powers, axis=1, keepdims=True)
    summed = jnp.dot(powers.astype(value.dtype), value, preferred_element_type=jnp.float32)
    summed = summed / total
    if width % LANES == 0:
        result = summed[:block]
        for head in range(1, heads):
            result = jnp.where(lane == head, summed[head * block : (head + 1) * block], result)
    else:
        result = summed[:, width:]
    mixed[...] = result.astype(mixed.dtype)


def gather_attend(table, queries, pieces, block, width):
    steps = table.shape[0]
    blocks = [piece.reshape(-1, block, piece.shape[-1]) for piece in pieces]
    counts = tuple(piece.shape[0] for piece in blocks)
    return pl.pallas_call(
        functools.partial(gather_attend_kernel, counts, width),
        grid_spec=pltpu.PrefetchScalarGridSpec(
            num_scalar_prefetch=1,
            grid=(steps,),
            in_specs=[pl.BlockSpec((block, width), lambda i, t: (i, 0))]
            + [pl.BlockSpec(memory_space=pl.ANY)] * len(blocks),
            out_specs=pl.BlockSpec((block, width), lambda i, t: (i, 0)),
            scratch_shapes=[
                pltpu.VMEM((sum(counts), block, blocks[0].shape[-1]), queries.dtype),
                pltpu.SemaphoreType.DMA,
            ],
        ),
        out_shape=jax.ShapeDtypeStruct(queries.shape, queries.dtype),
        name="gather_attend",
    )(table, queries, *blocks)


def norm_kernel(cores, width, at, *rest):
    pieces, gain, out = rest[:-2], rest[-2], rest[-1]
    ranks = len(pieces) // cores
    core, rank = at[0], at[1]
    parts = []
    square = 0.0
    for which in range(cores):
        for flip in range(ranks):
            part = pieces[which * ranks + flip][...].astype(jnp.float32)
            square = square + part * part
            parts.append((((rank ^ flip) * cores + (core ^ which)) * width, part))
    features = len(parts) * width
    mean_square = jnp.sum(square, axis=-1, keepdims=True) * (1.0 / features)
    factor = lax.rsqrt(mean_square + 1e-06)
    for column, part in parts:
        columns = pl.ds(pl.multiple_of(column, width), width)
        out[:, columns] = (part * factor * gain[:, columns]).astype(out.dtype)


def normalize(pieces, gain, core, rank, cores, width):
    ranks = len(pieces[0])
    rows = pieces[0][0].shape[0]
    flat = [piece for of_which in pieces for piece in of_which]
    features = ranks * cores * width
    if width % LANES == 0:
        step = min(rows, 256)
        return pl.pallas_call(
            functools.partial(norm_kernel, cores, width),
            grid_spec=pltpu.PrefetchScalarGridSpec(
                num_scalar_prefetch=1,
                grid=(rows // step,),
                in_specs=[pl.BlockSpec((step, width), lambda i, t: (i, 0))] * len(flat)
                + [pl.BlockSpec((1, features), lambda i, t: (0, 0))],
                out_specs=pl.BlockSpec((step, features), lambda i, t: (i, 0)),
            ),
            out_shape=jax.ShapeDtypeStruct((rows, features), flat[0].dtype),
            name="normalize",
        )(jnp.stack([core, rank]), *flat, gain[None])
    stacked = jnp.stack([jnp.stack(of_which) for of_which in pieces])
    stacked = stacked[core ^ jnp.arange(cores)][:, rank ^ jnp.arange(ranks)]
    restored = jnp.transpose(stacked, (2, 1, 0, 3)).reshape(rows, features).astype(jnp.float32)
    mean_square = jnp.mean(restored * restored, axis=-1, keepdims=True)
    return (restored * lax.rsqrt(mean_square + 1e-06) * gain).astype(flat[0].dtype)


def local(shape, queries, keys, values, matchings, patterns, gain):
    clusters, ranks = shape
    rows, features = queries.shape
    heads = features // HEAD_DIM // ranks
    cores = core_split(shape, features)
    width = heads // cores * HEAD_DIM
    cluster, rank = lax.axis_index("clus"), lax.axis_index("head")
    core = cluster % cores
    blocks = patterns.shape[1]
    block = rows * ranks // blocks
    rank_blocks = rows // block
    fast = cores == 2 and width == LANES and block == LANES and patterns.shape[2] % 2 == 0

    pairs, head_queries = split_heads(
        queries, keys, values, core, rank, ranks, cores, width, fast
    )
    chosen = [patterns[0]] + [swap(patterns, shape, which, 0)[0] for which in range(1, cores)]

    def moved(pieces):
        return [
            [
                swap(piece, shape, which, flip) if which or flip else piece
                for flip, piece in enumerate(of_which)
            ]
            for which, of_which in enumerate(pieces)
        ]

    pairs, head_queries = moved(pairs), moved(head_queries)

    bits = [cores << i for i in range((clusters // cores).bit_length() - 1)]
    span = max(1, ranks // 4)
    streams = []
    for which in range(cores):
        for start in range(0, ranks, span):
            group = pairs[which][start : start + span]
            gathered = {0: jnp.concatenate(group, axis=0) if span > 1 else group[0]}
            turn = (which + start // span) % 2
            for bit in bits[::-1] if turn else bits:
                gathered |= {
                    there | bit: swap(piece, shape, bit, 0)
                    for there, piece in gathered.items()
                }
            streams.append(
                [gathered[there].reshape(-1, block, 2 * width) for there in sorted(gathered)]
            )

    table = []
    for which in range(cores):
        source, number = chosen[which] // blocks, chosen[which] % blocks
        partner = jnp.broadcast_to(cluster ^ which, source.shape)
        for matching in range(matchings.shape[0]):
            partner = jnp.where(
                source == matching + 1, matchings[matching, cluster ^ which], partner
            )
        there = partner ^ cluster
        flip = (number // rank_blocks) ^ rank
        place = ((there % cores) * (ranks // span) + flip // span) * (clusters // cores)
        place = (place + there // cores) * span + flip % span
        table.append(place * rank_blocks + number % rank_blocks)
    table = jnp.concatenate(table, axis=0).astype(jnp.int32)

    if fast:
        at = jnp.stack([core, rank])
        held, total = None, clusters * blocks
        per_stream = clusters // cores * rank_blocks
        for flip in range(ranks // span):
            pieces, places = [], []
            for which in range(cores):
                stream = which * (ranks // span) + flip
                for number, piece in enumerate(streams[stream]):
                    pieces.append(piece)
                    places.append(stream * per_stream + number * piece.shape[0])
            held = hold(pieces, tuple(places), held, total)
        mixed = [[None] * ranks for _ in range(cores)]
        for flip in reversed(range(ranks)):
            results = attend(
                at, table, [head_queries[which][flip] for which in range(cores)], held, flip, blocks
            )
            for which in range(cores):
                mixed[which][flip] = results[which]
    else:
        order = [(which, flip) for which in range(cores) for flip in range(ranks)]
        stacked = jnp.concatenate([head_queries[which][flip] for which, flip in order], axis=0)
        rows_of = table.reshape(cores, ranks, rank_blocks, -1)[:, rank ^ jnp.arange(ranks)]
        result = gather_attend(
            rows_of.reshape(cores * blocks, -1),
            stacked,
            [piece for stream in streams for piece in stream],
            block,
            width,
        ).reshape(cores, ranks, rows, width)
        mixed = [list(of_which) for of_which in result]
    return normalize(moved(mixed), gain, core, rank, cores, width)


def core_split(shape, features):
    clusters, ranks = shape
    return 2 if features // HEAD_DIM // ranks % 2 == 0 and clusters % 2 == 0 else 1


def solution(mesh):
    shape = (mesh.shape["clus"], mesh.shape["head"])
    in_specs = (
        P(("clus", "head"), None),
        P(("clus", "head"), None),
        P(("clus", "head"), None),
        P(),
        P("clus", None, None),
        P(),
    )
    out_specs = P(("clus", "head"), None)

    def body(*args):
        return local(shape, *args)

    return jax.shard_map(body, mesh=mesh, in_specs=in_specs, out_specs=out_specs, check_vma=False)
```
